256 devices in a mesh: row: 8 (over z_lo, y), col: 16 (over z_hi, x), leaf: 2 (over core).
Axes of the slice: x: 4, y: 4, z: 8 (z_hi: 4, z_lo: 2; z = z_hi * 2 + z_lo), core: 2. Of those that a mesh axis runs over, the one named last changes fastest.
Arguments:
- front: float32 [16384, 16384], P('row', ('col', 'leaf')), may hold values from -6 to 6
- child: float32 [16384, 16384], P(('row', 'col', 'leaf')), may hold values from -6 to 6
- row_map: int32 [8, 8], P('row'), may hold values from 0 to 7, each once within a row
- col_map: int32 [64], replicated, may hold values from 0 to 63, each once
- x_fac: float32 [64, 16384], P('row', ('col', 'leaf')), may hold values from -0.75 to 0.75
- w_fac: float32 [64, 16384], P('row', ('col', 'leaf')), may hold values from -0.375 to 0.375
- v_fac: float32 [64, 16384], P(('col', 'leaf'), 'row'), may hold values from -6 to 6
- z_fac: float32 [64, 16384], P(('col', 'leaf'), 'row'), may hold values from -0.75 to 0.75
- dinv: float32 [256, 256], replicated, may hold values from -0.375 to 0.375
- pivots: int32 [256], replicated, may hold values from 0 to 255, each once
- rank_rows: int32 [64], P('row'), may hold values from 16 to 64
- rank_cols: int32 [64], P(('col', 'leaf')), may hold values from 16 to 64
- admissible: int32 [64, 64], P('row', ('col', 'leaf')), may hold values 0 or 1
Outputs:
- updated: float32 [16384, 16384], P('row', ('col', 'leaf'))
The draws below stay inside these ranges and needn't reach their ends.
Inputs may be any that keep to these rules, and one draw needn't show every extreme that they name: Each row of row_map orders the 8 tile rows of one group; col_map orders all 64 tile columns. `pivots`: A permutation of the panel's columns.
All inputs are finite; a program needn't handle non-finite values. No bound on the sum of `admissible` on one device may be relied on, other than what follows from the above.
Results may differ from the reference program's by a relative error of at most 0.0003.
Values sent between devices are 32-bit elements; how exact they have to be, the bound alone decides.
A program may use at most 128 MiB of HBM per device.

```python
import jax
import jax.numpy as jnp
from jax import lax

B = 256
RMAX = 64
RT = 8
NRT = 64
NCT = 64
MROWS = 16384
MCOLS = 16384
N_ROW = 8


def set_ends(entries, stream_key, least, high):
    extent = entries.shape
    spot = [jax.random.randint(jax.random.fold_in(stream_key, axis), (), 0, extent[axis]) for axis in range(len(extent))]
    entries = entries.at[tuple(spot)].set(least)
    longest = extent.index(max(extent))
    spot[longest] = (spot[longest] + 1) % extent[longest]
    return entries.at[tuple(spot)].set(high)


def block_scale(rng, shape, shards, least, high):
    def one(axis_at, blocks):
        draws = jax.random.uniform(jax.random.fold_in(jax.random.fold_in(rng, 6), axis_at), (blocks,), jnp.float32, least / len(shards), high / len(shards))
        return jnp.repeat(jnp.exp(draws), shape[axis_at] // blocks).reshape((-1,) + (1,) * (len(shape) - axis_at - 1))

    gain = one(*shards[0])
    for cut in shards[1:]:
        gain = gain * one(*cut)
    return gain


def noise(stream_key, dims, scale, most, shards=(), kind=jnp.bfloat16):
    level = block_scale(stream_key, dims, shards, -0.22, 0.18) if shards else 1.0
    array = jax.random.normal(stream_key, dims, jnp.float32) * scale * level
    return jnp.minimum(jnp.maximum(array, -most), most).astype(kind)


def setup_inputs(seed: int = 0) -> dict:
    seeds = jax.random.split(jax.random.key(seed), 14)
    return {
        "front": noise(seeds[0], (MROWS, MCOLS), 1.0, 6.0, ((0, 8), (1, 32)), jnp.float32),
        "child": noise(seeds[1], (MROWS, MCOLS), 1.0, 6.0, ((0, 256),), jnp.float32),
        "row_map": jax.vmap(lambda own: jax.random.permutation(own, RT))(jax.random.split(seeds[2], N_ROW)).reshape((N_ROW, RT)).astype(jnp.int32),
        "col_map": jax.random.permutation(seeds[3], NCT).astype(jnp.int32),
        "x_fac": noise(seeds[4], (NRT, RMAX * B), RMAX ** -0.5, 0.75, ((0, 8), (1, 32)), jnp.float32),
        "w_fac": noise(seeds[5], (NRT, RMAX * B), B ** -0.5, 0.375, ((0, 8), (1, 32)), jnp.float32),
        "v_fac": noise(seeds[6], (NCT, RMAX * B), 1.0, 6.0, ((0, 32), (1, 8)), jnp.float32),
        "z_fac": noise(seeds[7], (NCT, RMAX * B), RMAX ** -0.5, 0.75, ((0, 32), (1, 8)), jnp.float32),
        "dinv": noise(seeds[8], (B, B), B ** -0.5, 0.375, (), jnp.float32),
        "pivots": jax.random.permutation(seeds[9], B).astype(jnp.int32),
        "rank_rows": set_ends(jax.random.randint(seeds[10], (NRT,), RMAX // 4, RMAX + 1), jax.random.fold_in(seeds[10], 1), RMAX // 4, RMAX).astype(jnp.int32),
        "rank_cols": set_ends(jax.random.randint(seeds[11], (NCT,), RMAX // 4, RMAX + 1), jax.random.fold_in(seeds[11], 1), RMAX // 4, RMAX).astype(jnp.int32),
        "admissible": set_ends((jax.random.randint(seeds[12], (NRT, NCT), 0, 2) < 1).astype(jnp.int32), jax.random.fold_in(seeds[12], 1), 0, 1),
    }


def inverse_order(order):
    count = order.shape[0]
    return jnp.zeros((count,), jnp.int32).at[order].set(jnp.arange(count, dtype=jnp.int32))


def reference(front, child, row_map, col_map, x_fac, w_fac, v_fac, z_fac, dinv, pivots, rank_rows, rank_cols, admissible):
    highest = lax.Precision.HIGHEST
    tile = dinv.shape[0]
    nrt = x_fac.shape[0]
    nct = v_fac.shape[0]
    rank_max = x_fac.shape[1] // tile
    x_three = x_fac.reshape(nrt, rank_max, tile)
    w_three = w_fac.reshape(nrt, rank_max, tile)
    v_three = v_fac.reshape(nct, rank_max, tile)
    z_three = z_fac.reshape(nct, rank_max, tile)
    groups = row_map.shape[0]
    per_group = row_map.shape[1]
    dest_rows = (jnp.arange(groups, dtype=jnp.int32)[:, None] * per_group + row_map).reshape(-1)
    blocks = child.reshape(nrt, tile, nct, tile)
    blocks = jnp.take(blocks, inverse_order(dest_rows), axis=0)
    blocks = jnp.take(blocks, inverse_order(col_map), axis=2)
    relaid = blocks.reshape(nrt * tile, nct * tile)
    dv = jnp.einsum('kb,jrb->jkr', dinv, v_three, precision=highest)
    permuted = jnp.take(w_three, pivots, axis=2)
    rank_index = jnp.arange(rank_max, dtype=jnp.int32)

    def one_row(items):
        x_row, w_row, rank_row, adm_row = items
        core = jnp.einsum('rk,jks->jrs', w_row, dv, precision=highest)
        dense_tile = (adm_row == 0)[:, None]
        keep_rows = (rank_index[None, :] < rank_row) | dense_tile
        keep_cols = (rank_index[None, :] < rank_cols[:, None]) | dense_tile
        core = jnp.where(keep_rows[:, :, None] & keep_cols[:, None, :], core, jnp.float32(0.0))
        left = jnp.einsum('rb,jrs->jbs', x_row, core, precision=highest)
        product = jnp.einsum('jbs,jsc->bjc', left, z_three, precision=highest)
        return product.reshape(tile, nct * tile)

    update = lax.map(one_row, (x_three, permuted, rank_rows, admissible)).reshape(nrt * tile, nct * tile)
    return front + relaid - update
```

```python
import jax
import jax.numpy as jnp
from jax import lax
from jax.experimental import pallas as pl
from jax.experimental.pallas import tpu as pltpu
from jax.sharding import PartitionSpec as P

TILE = 256
RMAX = 64
MESH = pl.DeviceIdType.MESH
HIGHEST = lax.Precision.HIGHEST


def peer_of(row, col, leaf):
    return {"row": row, "col": col, "leaf": leaf}


def exchange_kernel(
    inv_col_h,
    rank_rows_h,
    rank_cols_h,
    admissible_h,
    child,
    front,
    x_fac_h,
    w_fac_h,
    v_fac_h,
    z_fac_h,
    dinv_h,
    pivots_h,
    arrived,
    front_v,
    inv_col,
    rank_rows,
    rank_cols,
    admissible,
    x_fac,
    w_fac,
    v_fac,
    z_fac,
    dinv,
    pivots,
    child_v,
    out_v,
    xw,
    vz,
    v_cat,
    z_diag,
    dv,
    local_sem,
    small_sem,
    a2a_send,
    a2a_recv,
    xw_send,
    xw_recv,
    vz_send,
    vz_recv,
):
    row, col, leaf = lax.axis_index("row"), lax.axis_index("col"), lax.axis_index("leaf")
    z_low, y = row // 4, row % 4
    z_high, x = col // 4, col % 4
    me = col * 2 + leaf

    def load_tile(c, carry):
        tile = child.at[:, pl.ds(pl.multiple_of(c * TILE, TILE), TILE)]
        pltpu.make_async_copy(tile, child_v.at[c], local_sem.at[0]).start()
        return carry

    load_front = pltpu.make_async_copy(front, front_v, local_sem.at[1])
    small = [
        pltpu.make_async_copy(source, target, small_sem.at[k])
        for k, (source, target) in enumerate(
            (
                (inv_col_h, inv_col),
                (x_fac_h, x_fac),
                (w_fac_h, w_fac),
                (v_fac_h, v_fac),
                (z_fac_h, z_fac),
                (dinv_h, dinv),
                (pivots_h, pivots),
                (rank_rows_h, rank_rows),
                (rank_cols_h, rank_cols),
                (admissible_h, admissible),
            )
        )
    ]
    for copy in small[:5]:
        copy.start()
    lax.fori_loop(0, 64, load_tile, 0)
    for copy in small[5:]:
        copy.start()

    barrier = pltpu.get_barrier_semaphore()

    def greet(m, carry):
        to = peer_of(
            row,
            ((z_high + m // 8) % 4) * 4 + (x + (m // 2) % 4) % 4,
            (leaf + m % 2) % 2,
        )
        pl.semaphore_signal(barrier, inc=1, device_id=to, device_id_type=MESH)
        return carry

    lax.fori_loop(1, 32, greet, 0)
    pl.semaphore_signal(
        barrier, inc=1, device_id=peer_of((1 - z_low) * 4 + y, col, leaf), device_id_type=MESH
    )
    for step in range(1, 4):
        pl.semaphore_signal(
            barrier,
            inc=1,
            device_id=peer_of(z_low * 4 + (y + step) % 4, col, leaf),
            device_id_type=MESH,
        )

    for copy in small[:5]:
        copy.wait()
    spot = leaf * 16 + x * 4 + z_high
    for c in range(4):
        lanes = slice(c * 128, (c + 1) * 128)
        xw[pl.ds(pl.multiple_of(spot * 64 + c * 16, 16), 8), :] = x_fac[:, lanes]
        xw[pl.ds(pl.multiple_of(spot * 64 + c * 16 + 8, 8), 8), :] = w_fac[:, lanes]
    place = y * 2 + z_low
    for q in range(8):
        lanes = slice(q * TILE, (q + 1) * TILE)
        for j in range(2):
            vz[place, 0, j, q : q + 1, :] = v_fac[j : j + 1, lanes]
            vz[place, 1, j, q : q + 1, :] = z_fac[j : j + 1, lanes]

    pl.semaphore_wait(barrier, 35)

    def xw_copy(start, count, stage, to):
        part = xw.at[pl.ds(pl.multiple_of(start * 64, 64), count * 64), :]
        return pltpu.make_async_remote_copy(
            src_ref=part,
            dst_ref=part,
            send_sem=xw_send.at[stage],
            recv_sem=xw_recv.at[stage],
            device_id=to,
            device_id_type=MESH,
        )

    def vz_copy(start, count, stage, to):
        part = vz.at[pl.ds(start, count)]
        return pltpu.make_async_remote_copy(
            src_ref=part,
            dst_ref=part,
            send_sem=vz_send.at[stage],
            recv_sem=vz_recv.at[stage],
            device_id=to,
            device_id_type=MESH,
        )

    xw_z = [
        xw_copy(spot, 1, 0, peer_of(row, ((z_high + s) % 4) * 4 + x, leaf)) for s in (2, 1, 3)
    ]
    xw_x = [
        xw_copy(leaf * 16 + x * 4, 4, 1, peer_of(row, z_high * 4 + (x + s) % 4, leaf))
        for s in (2, 1, 3)
    ]
    xw_leaf = [xw_copy(leaf * 16, 16, 2, peer_of(row, col, 1 - leaf))]
    vz_z = [vz_copy(place, 1, 0, peer_of((1 - z_low) * 4 + y, col, leaf))]
    vz_y = [
        vz_copy(y * 2, 2, 1, peer_of(z_low * 4 + (y + s) % 4, col, leaf)) for s in (2, 1, 3)
    ]

    for copy in xw_z + vz_z:
        copy.start()
    pltpu.make_async_copy(child_v, child_v, local_sem.at[0]).wait()
    load_front.start()

    def place_tiles(slot):
        for half in range(2):
            source = inv_col[slot * 2 + half]
            out_v[slot, :, half * TILE : (half + 1) * TILE] = child_v[source]

    def block_copy(m, dz):
        z_to, x_to, leaf_to = (z_high + dz) % 4, (x + m // 2) % 4, (leaf + m % 2) % 2
        slot = (z_to * 4 + x_to) * 2 + leaf_to
        return slot, pltpu.make_async_remote_copy(
            src_ref=out_v.at[slot],
            dst_ref=arrived.at[me],
            send_sem=a2a_send,
            recv_sem=a2a_recv,
            device_id=peer_of(row, z_to * 4 + x_to, leaf_to),
            device_id_type=MESH,
        )

    def send_blocks(first, dz):
        def one(m, carry):
            slot, copy = block_copy(m, dz)
            place_tiles(slot)
            copy.start()
            return carry

        lax.fori_loop(first, 8, one, 0)

    def settle_xw(pieces, stage):
        xw_copy(0, pieces, stage, peer_of(row, col, 1 - leaf)).wait()

    def settle_vz(pieces, stage):
        vz_copy(0, pieces, stage, peer_of(row, col, 1 - leaf)).wait()

    send_blocks(0, 2)
    settle_xw(3, 0)
    settle_vz(1, 0)
    for copy in xw_x + vz_y:
        copy.start()
    send_blocks(0, 1)
    settle_xw(12, 1)
    settle_vz(6, 1)
    for copy in xw_leaf:
        copy.start()
    send_blocks(0, 3)
    send_blocks(1, 0)
    place_tiles(me)
    arrived[me] = out_v[me]
    for copy in small[5:]:
        copy.wait()

    places = lax.broadcasted_iota(jnp.int32, (TILE, TILE), 0)
    chosen = jnp.where(places == pivots[...], jnp.float32(1.0), jnp.float32(0.0))
    permuted = jnp.dot(chosen, dinv[...], precision=HIGHEST, preferred_element_type=jnp.float32)
    z_diag[...] = jnp.zeros_like(z_diag)
    for j in range(2):
        for g in range(8):
            at = (g % 4) * 2 + g // 4
            v_cat[j * RMAX + g * 8 : j * RMAX + g * 8 + 8, :] = vz[at, 0, j]
            z_diag[j * RMAX + g * 8 : j * RMAX + g * 8 + 8, j * TILE : (j + 1) * TILE] = vz[
                at, 1, j
            ]
    dv[...] = lax.dot_general(
        permuted,
        v_cat[...],
        (((1,), (1,)), ((), ())),
        precision=HIGHEST,
        preferred_element_type=jnp.float32,
    )

    settle_xw(16, 2)
    load_front.wait()

    at = lax.broadcasted_iota(jnp.int32, (RMAX, 2 * RMAX), 0)
    piece = at % 32
    rank_row = (piece % 4) * 16 + ((piece // 4) % 4) * 4 + (piece // 16) * 2 + at // 32
    lane = lax.broadcasted_iota(jnp.int32, (RMAX, 2 * RMAX), 1)
    rank_col = lane % RMAX
    second = lane >= RMAX
    limit_col = jnp.where(second, rank_cols[1], rank_cols[0])

    def gathered(first):
        parts = [xw[pl.ds(first + c * 16, 32, stride=64), :] for c in range(4)]
        return jnp.concatenate(
            [jnp.concatenate(parts[:2], axis=1), jnp.concatenate(parts[2:], axis=1)], axis=0
        )

    def tile_row(i, carry):
        x_rows, w_rows = gathered(i), gathered(i + 8)
        core = jnp.dot(w_rows, dv[...], precision=HIGHEST, preferred_element_type=jnp.float32)
        dense = jnp.where(second, admissible[1, i], admissible[0, i]) == 0
        keep = dense | ((rank_row < rank_rows[i]) & (rank_col < limit_col))
        kept = jnp.where(keep, core, jnp.float32(0.0))
        left = lax.dot_general(
            x_rows,
            kept,
            (((0,), (0,)), ((), ())),
            precision=HIGHEST,
            preferred_element_type=jnp.float32,
        )
        update = jnp.dot(
            left, z_diag[...], precision=HIGHEST, preferred_element_type=jnp.float32
        )
        rows = pl.ds(pl.multiple_of(i * TILE, TILE), TILE)
        front_v[rows, :] = front_v[rows, :] - update
        return carry

    lax.fori_loop(0, 8, tile_row, 0)

    pltpu.make_async_remote_copy(
        src_ref=out_v.at[pl.ds(0, 31)],
        dst_ref=arrived.at[pl.ds(0, 31)],
        send_sem=a2a_send,
        recv_sem=a2a_recv,
        device_id=peer_of(row, col, 1 - leaf),
        device_id_type=MESH,
    ).wait()


def add_kernel(row_map, partial, arrived, updated):
    t = pl.program_id(0)
    source = 0
    for a in range(8):
        source = source + jnp.where(row_map[0, a] == t, a, 0)
    updated[...] = (
        partial[pl.ds(pl.multiple_of(t * TILE, TILE), TILE), :]
        + arrived[pl.ds(pl.multiple_of(source * TILE, TILE), TILE), :]
    )


def on_device(
    front,
    child,
    row_map,
    col_map,
    x_fac,
    w_fac,
    v_fac,
    z_fac,
    dinv,
    pivots,
    rank_rows,
    rank_cols,
    admissible,
):
    tiles = col_map.shape[0]
    order = jnp.arange(tiles, dtype=jnp.int32)
    inv_col = jnp.sum(
        jnp.where(col_map[None, :] == order[:, None], order[None, :], 0), axis=1, dtype=jnp.int32
    )
    vmem = pl.BlockSpec(memory_space=pltpu.VMEM)
    hbm = pl.BlockSpec(memory_space=pltpu.HBM)
    f32 = jnp.float32
    arrived, partial = pl.pallas_call(
        exchange_kernel,
        name="exchange",
        out_shape=(
            jax.ShapeDtypeStruct((32, 64, 512), f32),
            jax.ShapeDtypeStruct(front.shape, f32),
        ),
        in_specs=[hbm] * 12,
        out_specs=(vmem, vmem),
        scratch_shapes=[
            pltpu.SMEM((tiles,), jnp.int32),
            pltpu.SMEM(rank_rows.shape, jnp.int32),
            pltpu.SMEM(rank_cols.shape, jnp.int32),
            pltpu.SMEM(admissible.shape[::-1], jnp.int32),
            pltpu.VMEM(x_fac.shape, f32),
            pltpu.VMEM(w_fac.shape, f32),
            pltpu.VMEM(v_fac.shape, f32),
            pltpu.VMEM(z_fac.shape, f32),
            pltpu.VMEM(dinv.shape, f32),
            pltpu.VMEM((1, TILE), jnp.int32),
            pltpu.VMEM((tiles, child.shape[0], TILE), f32),
            pltpu.VMEM((32, 64, 512), f32),
            pltpu.VMEM((32 * 64, 128), f32),
            pltpu.VMEM((8, 2, 2, 8, TILE), f32),
            pltpu.VMEM((2 * RMAX, TILE), f32),
            pltpu.VMEM((2 * RMAX, 2 * TILE), f32),
            pltpu.VMEM((TILE, 2 * RMAX), f32),
            pltpu.SemaphoreType.DMA((2,)),
            pltpu.SemaphoreType.DMA((10,)),
            pltpu.SemaphoreType.DMA,
            pltpu.SemaphoreType.DMA,
            pltpu.SemaphoreType.DMA((3,)),
            pltpu.SemaphoreType.DMA((3,)),
            pltpu.SemaphoreType.DMA((2,)),
            pltpu.SemaphoreType.DMA((2,)),
        ],
        compiler_params=pltpu.CompilerParams(
            collective_id=0, has_side_effects=True, vmem_limit_bytes=32 << 20
        ),
    )(*(pltpu.with_memory_space_constraint(a, pltpu.HBM) for a in (
        inv_col,
        rank_rows,
        rank_cols,
        admissible.T,
        child,
        front,
        x_fac,
        w_fac,
        v_fac,
        z_fac,
        dinv,
        pivots.reshape(1, TILE),
    )))

    block = (TILE, 512)
    return pl.pallas_call(
        add_kernel,
        name="extend_add",
        out_shape=jax.ShapeDtypeStruct(front.shape, f32),
        grid_spec=pltpu.PrefetchScalarGridSpec(
            num_scalar_prefetch=1,
            grid=(8,),
            in_specs=[vmem, vmem],
            out_specs=pl.BlockSpec(block, lambda t, mapping: (t, 0)),
        ),
        compiler_params=pltpu.CompilerParams(vmem_limit_bytes=8 << 20),
        cost_estimate=pl.CostEstimate(
            flops=1 << 20, bytes_accessed=12 << 20, transcendentals=0
        ),
    )(row_map, partial, arrived.reshape(front.shape))


def solution(mesh):
    return jax.shard_map(
        on_device,
        mesh=mesh,
        in_specs=(
            P("row", ("col", "leaf")),
            P(("row", "col", "leaf"), None),
            P("row", None),
            P(),
            P("row", ("col", "leaf")),
            P("row", ("col", "leaf")),
            P(("col", "leaf"), "row"),
            P(("col", "leaf"), "row"),
            P(),
            P(),
            P("row"),
            P(("col", "leaf")),
            P("row", ("col", "leaf")),
        ),
        out_specs=P("row", ("col", "leaf")),
        check_vma=False,
    )
```

```python
import jax
import jax.numpy as jnp
from jax import lax
from jax.experimental import pallas as pl
from jax.experimental.pallas import tpu as pltpu
from jax.sharding import PartitionSpec as P

TILE = 256
RMAX = 64
MESH = pl.DeviceIdType.MESH
HIGHEST = lax.Precision.HIGHEST


def peer_of(row, col, leaf):
    return {"row": row, "col": col, "leaf": leaf}


def exchange_kernel(
    col_map_h,
    row_map_h,
    rank_rows_h,
    rank_cols_h,
    admissible_h,
    child,
    front,
    x_fac_h,
    w_fac_h,
    v_fac_h,
    z_fac_h,
    dinv_h,
    pivots_h,
    arrived,
    col_map,
    row_map,
    rank_rows,
    rank_cols,
    admissible,
    x_fac,
    w_fac,
    v_fac,
    z_fac,
    dinv,
    pivots,
    child_v,
    out_v,
    front_v,
    xw,
    vz,
    v_cat,
    z_diag,
    dv,
    local_sem,
    small_sem,
    a2a_send,
    a2a_recv,
    xw_send,
    xw_recv,
    vz_send,
    vz_recv,
):
    row, col, leaf = lax.axis_index("row"), lax.axis_index("col"), lax.axis_index("leaf")
    z_low, y = row // 4, row % 4
    z_high, x = col // 4, col % 4
    me = col * 2 + leaf

    def load_tile(c, carry):
        tile = child.at[:, pl.ds(pl.multiple_of(c * TILE, TILE), TILE)]
        pltpu.make_async_copy(tile, child_v.at[c], local_sem.at[0]).start()
        return carry

    load_front = pltpu.make_async_copy(front, front_v, local_sem.at[1])
    small = [
        pltpu.make_async_copy(source, target, small_sem.at[k])
        for k, (source, target) in enumerate(
            (
                (col_map_h, col_map),
                (x_fac_h, x_fac),
                (w_fac_h, w_fac),
                (v_fac_h, v_fac),
                (z_fac_h, z_fac),
                (dinv_h, dinv),
                (pivots_h, pivots),
                (rank_rows_h, rank_rows),
                (rank_cols_h, rank_cols),
                (admissible_h, admissible),
                (row_map_h, row_map),
            )
        )
    ]
    barrier = pltpu.get_barrier_semaphore()

    def greet(m, carry):
        to = peer_of(
            row,
            ((z_high + m // 8) % 4) * 4 + (x + (m // 2) % 4) % 4,
            (leaf + m % 2) % 2,
        )
        pl.semaphore_signal(barrier, inc=1, device_id=to, device_id_type=MESH)
        return carry

    lax.fori_loop(1, 32, greet, 0)
    pl.semaphore_signal(
        barrier, inc=1, device_id=peer_of((1 - z_low) * 4 + y, col, leaf), device_id_type=MESH
    )
    for step in range(1, 4):
        pl.semaphore_signal(
            barrier,
            inc=1,
            device_id=peer_of(z_low * 4 + (y + step) % 4, col, leaf),
            device_id_type=MESH,
        )

    for copy in small[:5]:
        copy.start()
    lax.fori_loop(0, 64, load_tile, 0)
    for copy in small[5:]:
        copy.start()

    for copy in small[:5]:
        copy.wait()
    spot = leaf * 16 + x * 4 + z_high
    for c in range(4):
        lanes = slice(c * 128, (c + 1) * 128)
        xw[pl.ds(pl.multiple_of(spot * 64 + c * 16, 16), 8), :] = x_fac[:, lanes]
        xw[pl.ds(pl.multiple_of(spot * 64 + c * 16 + 8, 8), 8), :] = w_fac[:, lanes]
    place = y * 2 + z_low
    for q in range(8):
        lanes = slice(q * TILE, (q + 1) * TILE)
        for j in range(2):
            vz[place, 0, j, q : q + 1, :] = v_fac[j : j + 1, lanes]
            vz[place, 1, j, q : q + 1, :] = z_fac[j : j + 1, lanes]

    pl.semaphore_wait(barrier, 35)

    def xw_copy(start, count, stage, to):
        part = xw.at[pl.ds(pl.multiple_of(start * 64, 64), count * 64), :]
        return pltpu.make_async_remote_copy(
            src_ref=part,
            dst_ref=part,
            send_sem=xw_send.at[stage],
            recv_sem=xw_recv.at[stage],
            device_id=to,
            device_id_type=MESH,
        )

    def vz_copy(start, count, stage, to):
        part = vz.at[pl.ds(start, count)]
        return pltpu.make_async_remote_copy(
            src_ref=part,
            dst_ref=part,
            send_sem=vz_send.at[stage],
            recv_sem=vz_recv.at[stage],
            device_id=to,
            device_id_type=MESH,
        )

    xw_z = [
        xw_copy(spot, 1, 0, peer_of(row, ((z_high + s) % 4) * 4 + x, leaf)) for s in (2, 1, 3)
    ]
    xw_x = [
        xw_copy(leaf * 16 + x * 4, 4, 1, peer_of(row, z_high * 4 + (x + s) % 4, leaf))
        for s in (2, 1, 3)
    ]
    xw_leaf = [xw_copy(leaf * 16, 16, 2, peer_of(row, col, 1 - leaf))]
    vz_z = [vz_copy(place, 1, 0, peer_of((1 - z_low) * 4 + y, col, leaf))]
    vz_y = [
        vz_copy(y * 2, 2, 1, peer_of(z_low * 4 + (y + s) % 4, col, leaf)) for s in (2, 1, 3)
    ]

    for copy in xw_z + vz_z:
        copy.start()
    pltpu.make_async_copy(child_v, child_v, local_sem.at[0]).wait()
    load_front.start()

    def place_tiles(slot):
        def find(b, found):
            to = col_map[b]
            return tuple(jnp.where(to == slot * 2 + h, b, found[h]) for h in range(2))

        sources = lax.fori_loop(0, 64, find, (0, 0), unroll=8)
        for half, source in enumerate(sources):
            out_v[slot, :, half * TILE : (half + 1) * TILE] = child_v[source]

    def block_copy(m, dz):
        z_to, x_to, leaf_to = (z_high + dz) % 4, (x + m // 2) % 4, (leaf + m % 2) % 2
        slot = (z_to * 4 + x_to) * 2 + leaf_to
        return slot, pltpu.make_async_remote_copy(
            src_ref=out_v.at[slot],
            dst_ref=arrived.at[me],
            send_sem=a2a_send,
            recv_sem=a2a_recv,
            device_id=peer_of(row, z_to * 4 + x_to, leaf_to),
            device_id_type=MESH,
        )

    def send_blocks(first, dz):
        def one(m, carry):
            slot, copy = block_copy(m, dz)
            place_tiles(slot)
            copy.start()
            return carry

        lax.fori_loop(first, 8, one, 0)

    def settle_xw(pieces, stage):
        xw_copy(0, pieces, stage, peer_of(row, col, 1 - leaf)).wait()

    def settle_vz(pieces, stage):
        vz_copy(0, pieces, stage, peer_of(row, col, 1 - leaf)).wait()

    send_blocks(0, 2)
    settle_xw(3, 0)
    settle_vz(1, 0)
    for copy in xw_x + vz_y:
        copy.start()
    send_blocks(0, 1)
    settle_xw(12, 1)
    settle_vz(6, 1)
    for copy in xw_leaf:
        copy.start()
    send_blocks(0, 3)
    send_blocks(1, 0)
    place_tiles(me)
    arrived[me] = out_v[me]
    for copy in small[5:]:
        copy.wait()

    places = lax.broadcasted_iota(jnp.int32, (TILE, TILE), 0)
    chosen = jnp.where(places == pivots[...], jnp.float32(1.0), jnp.float32(0.0))
    permuted = jnp.dot(chosen, dinv[...], precision=HIGHEST, preferred_element_type=jnp.float32)
    z_diag[...] = jnp.zeros_like(z_diag)
    for j in range(2):
        for g in range(8):
            at = (g % 4) * 2 + g // 4
            v_cat[j * RMAX + g * 8 : j * RMAX + g * 8 + 8, :] = vz[at, 0, j]
            z_diag[j * RMAX + g * 8 : j * RMAX + g * 8 + 8, j * TILE : (j + 1) * TILE] = vz[
                at, 1, j
            ]
    dv[...] = lax.dot_general(
        permuted,
        v_cat[...],
        (((1,), (1,)), ((), ())),
        precision=HIGHEST,
        preferred_element_type=jnp.float32,
    )

    settle_xw(16, 2)
    load_front.wait()

    at = lax.broadcasted_iota(jnp.int32, (RMAX, 2 * RMAX), 0)
    piece = at % 32
    rank_row = (piece % 4) * 16 + ((piece // 4) % 4) * 4 + (piece // 16) * 2 + at // 32
    lane = lax.broadcasted_iota(jnp.int32, (RMAX, 2 * RMAX), 1)
    rank_col = lane % RMAX
    second = lane >= RMAX
    limit_col = jnp.where(second, rank_cols[1], rank_cols[0])

    def gathered(first):
        parts = [xw[pl.ds(first + c * 16, 32, stride=64), :] for c in range(4)]
        return jnp.concatenate(
            [jnp.concatenate(parts[:2], axis=1), jnp.concatenate(parts[2:], axis=1)], axis=0
        )

    def tile_row(i, carry):
        x_rows, w_rows = gathered(i), gathered(i + 8)
        core = jnp.dot(w_rows, dv[...], precision=HIGHEST, preferred_element_type=jnp.float32)
        dense = jnp.where(second, admissible[1, i], admissible[0, i]) == 0
        keep = dense | ((rank_row < rank_rows[i]) & (rank_col < limit_col))
        kept = jnp.where(keep, core, jnp.float32(0.0))
        left = lax.dot_general(
            x_rows,
            kept,
            (((0,), (0,)), ((), ())),
            precision=HIGHEST,
            preferred_element_type=jnp.float32,
        )
        update = jnp.dot(
            left, z_diag[...], precision=HIGHEST, preferred_element_type=jnp.float32
        )
        rows = pl.ds(i * 4, 4)
        front_v[rows] = front_v[rows] - update.reshape(4, TILE // 4, 2 * TILE)
        return carry

    lax.fori_loop(0, 8, tile_row, 0)

    pltpu.make_async_remote_copy(
        src_ref=out_v.at[pl.ds(0, 31)],
        dst_ref=arrived.at[pl.ds(0, 31)],
        send_sem=a2a_send,
        recv_sem=a2a_recv,
        device_id=peer_of(row, col, 1 - leaf),
        device_id_type=MESH,
    ).wait()

    for a in range(8):
        to = row_map[0, a]
        for k in range(4):
            arrived[a * 4 + k] = arrived[a * 4 + k] + front_v[to * 4 + k]


def place_kernel(row_map, summed, updated, sem):
    copies = []
    for a in range(8):
        rows = pl.ds(pl.multiple_of(row_map[0, a] * TILE, TILE), TILE)
        copies.append(
            pltpu.make_async_copy(
                summed.at[a * TILE : (a + 1) * TILE], updated.at[rows], sem.at[a]
            )
        )
    for copy in copies:
        copy.start()
    for copy in copies:
        copy.wait()


def on_device(
    front,
    child,
    row_map,
    col_map,
    x_fac,
    w_fac,
    v_fac,
    z_fac,
    dinv,
    pivots,
    rank_rows,
    rank_cols,
    admissible,
):
    tiles = col_map.shape[0]
    vmem = pl.BlockSpec(memory_space=pltpu.VMEM)
    hbm = pl.BlockSpec(memory_space=pltpu.HBM)
    f32 = jnp.float32
    summed = pl.pallas_call(
        exchange_kernel,
        name="exchange",
        out_shape=jax.ShapeDtypeStruct((32, 64, 512), f32),
        in_specs=[hbm] * 13,
        out_specs=vmem,
        scratch_shapes=[
            pltpu.SMEM((tiles,), jnp.int32),
            pltpu.SMEM(row_map.shape, jnp.int32),
            pltpu.SMEM(rank_rows.shape, jnp.int32),
            pltpu.SMEM(rank_cols.shape, jnp.int32),
            pltpu.SMEM(admissible.shape[::-1], jnp.int32),
            pltpu.VMEM(x_fac.shape, f32),
            pltpu.VMEM(w_fac.shape, f32),
            pltpu.VMEM(v_fac.shape, f32),
            pltpu.VMEM(z_fac.shape, f32),
            pltpu.VMEM(dinv.shape, f32),
            pltpu.VMEM((1, TILE), jnp.int32),
            pltpu.VMEM((tiles, child.shape[0], TILE), f32),
            pltpu.VMEM((32, 64, 512), f32),
            pltpu.VMEM((32, 64, 512), f32),
            pltpu.VMEM((32 * 64, 128), f32),
            pltpu.VMEM((8, 2, 2, 8, TILE), f32),
            pltpu.VMEM((2 * RMAX, TILE), f32),
            pltpu.VMEM((2 * RMAX, 2 * TILE), f32),
            pltpu.VMEM((TILE, 2 * RMAX), f32),
            pltpu.SemaphoreType.DMA((2,)),
            pltpu.SemaphoreType.DMA((11,)),
            pltpu.SemaphoreType.DMA,
            pltpu.SemaphoreType.DMA,
            pltpu.SemaphoreType.DMA((3,)),
            pltpu.SemaphoreType.DMA((3,)),
            pltpu.SemaphoreType.DMA((2,)),
            pltpu.SemaphoreType.DMA((2,)),
        ],
        compiler_params=pltpu.CompilerParams(
            collective_id=0, has_side_effects=True, vmem_limit_bytes=32 << 20
        ),
    )(*(pltpu.with_memory_space_constraint(a, pltpu.HBM) for a in (
        col_map,
        row_map,
        rank_rows,
        rank_cols,
        admissible.T,
        child,
        front.reshape(32, 64, 512),
        x_fac,
        w_fac,
        v_fac,
        z_fac,
        dinv,
        pivots.reshape(1, TILE),
    )))

    return pl.pallas_call(
        place_kernel,
        name="place_rows",
        out_shape=jax.ShapeDtypeStruct(front.shape, f32),
        in_specs=[pl.BlockSpec(memory_space=pltpu.SMEM), vmem],
        out_specs=hbm,
        scratch_shapes=[pltpu.SemaphoreType.DMA((8,))],
        compiler_params=pltpu.CompilerParams(vmem_limit_bytes=8 << 20),
    )(row_map, summed.reshape(front.shape))


def solution(mesh):
    return jax.shard_map(
        on_device,
        mesh=mesh,
        in_specs=(
            P("row", ("col", "leaf")),
            P(("row", "col", "leaf"), None),
            P("row", None),
            P(),
            P("row", ("col", "leaf")),
            P("row", ("col", "leaf")),
            P(("col", "leaf"), "row"),
            P(("col", "leaf"), "row"),
            P(),
            P(),
            P("row"),
            P(("col", "leaf")),
            P("row", ("col", "leaf")),
        ),
        out_specs=P("row", ("col", "leaf")),
        check_vma=False,
    )
```

```python
import jax
import jax.numpy as jnp
from jax import lax
from jax.experimental import pallas as pl
from jax.experimental.pallas import tpu as pltpu
from jax.sharding import PartitionSpec as P

TILE = 256
RMAX = 64
MESH = pl.DeviceIdType.MESH
PARTS = 2
HIGHEST = lax.Precision.HIGHEST


def peer_of(row, col, leaf):
    return {"row": row, "col": col, "leaf": leaf}


def exchange_kernel(
    col_map_h,
    row_map_h,
    rank_rows_h,
    rank_cols_h,
    admissible_h,
    child,
    front,
    x_fac_h,
    w_fac_h,
    v_fac_h,
    z_fac_h,
    dinv_h,
    pivots_h,
    arrived,
    front_v,
    col_map,
    row_map,
    rank_rows,
    rank_cols,
    admissible,
    x_fac,
    w_fac,
    v_fac,
    z_fac,
    dinv,
    pivots,
    child_v,
    out_v,
    xw,
    vz,
    v_cat,
    z_diag,
    dv,
    local_sem,
    small_sem,
    a2a_send,
    a2a_recv,
    xw_send,
    xw_recv,
    vz_send,
    vz_recv,
):
    row, col, leaf = lax.axis_index("row"), lax.axis_index("col"), lax.axis_index("leaf")
    z_low, y = row // 4, row % 4
    z_high, x = col // 4, col % 4
    me = col * 2 + leaf

    def load_tile(c, carry):
        tile = child.at[:, pl.ds(pl.multiple_of(c * TILE, TILE), TILE)]
        pltpu.make_async_copy(tile, child_v.at[c], local_sem.at[0]).start()
        return carry

    load_front = pltpu.make_async_copy(front, front_v, local_sem.at[1])
    small = [
        pltpu.make_async_copy(source, target, small_sem.at[k])
        for k, (source, target) in enumerate(
            (
                (col_map_h, col_map),
                (x_fac_h, x_fac),
                (w_fac_h, w_fac),
                (v_fac_h, v_fac),
                (z_fac_h, z_fac),
                (dinv_h, dinv),
                (pivots_h, pivots),
                (rank_rows_h, rank_rows),
                (rank_cols_h, rank_cols),
                (admissible_h, admissible),
                (row_map_h, row_map),
            )
        )
    ]
    barrier = pltpu.get_barrier_semaphore()

    def greet(m, carry):
        to = peer_of(
            row,
            ((z_high + m // 8) % 4) * 4 + (x + (m // 2) % 4) % 4,
            (leaf + m % 2) % 2,
        )
        pl.semaphore_signal(barrier, inc=1, device_id=to, device_id_type=MESH)
        return carry

    lax.fori_loop(1, 32, greet, 0)
    pl.semaphore_signal(
        barrier, inc=1, device_id=peer_of((1 - z_low) * 4 + y, col, leaf), device_id_type=MESH
    )
    for step in range(1, 4):
        pl.semaphore_signal(
            barrier,
            inc=1,
            device_id=peer_of(z_low * 4 + (y + step) % 4, col, leaf),
            device_id_type=MESH,
        )

    for copy in small[:5]:
        copy.start()
    lax.fori_loop(0, 64, load_tile, 0)
    for copy in small[5:]:
        copy.start()

    for copy in small[:5]:
        copy.wait()
    spot = leaf * 16 + x * 4 + z_high
    for c in range(4):
        lanes = slice(c * 128, (c + 1) * 128)
        xw[pl.ds(pl.multiple_of(spot * 64 + c * 16, 16), 8), :] = x_fac[:, lanes]
        xw[pl.ds(pl.multiple_of(spot * 64 + c * 16 + 8, 8), 8), :] = w_fac[:, lanes]
    place = y * 2 + z_low
    for q in range(8):
        lanes = slice(q * TILE, (q + 1) * TILE)
        for j in range(2):
            vz[place, 0, j, q : q + 1, :] = v_fac[j : j + 1, lanes]
            vz[place, 1, j, q : q + 1, :] = z_fac[j : j + 1, lanes]

    pl.semaphore_wait(barrier, 35)

    def xw_copy(start, count, stage, to):
        part = xw.at[pl.ds(pl.multiple_of(start * 64, 64), count * 64), :]
        return pltpu.make_async_remote_copy(
            src_ref=part,
            dst_ref=part,
            send_sem=xw_send.at[stage],
            recv_sem=xw_recv.at[stage],
            device_id=to,
            device_id_type=MESH,
        )

    def vz_copy(start, count, stage, to):
        part = vz.at[pl.ds(start, count)]
        return pltpu.make_async_remote_copy(
            src_ref=part,
            dst_ref=part,
            send_sem=vz_send.at[stage],
            recv_sem=vz_recv.at[stage],
            device_id=to,
            device_id_type=MESH,
        )

    xw_z = [
        xw_copy(spot, 1, 0, peer_of(row, ((z_high + s) % 4) * 4 + x, leaf)) for s in (2, 1, 3)
    ]
    xw_x = [
        xw_copy(leaf * 16 + x * 4, 4, 1, peer_of(row, z_high * 4 + (x + s) % 4, leaf))
        for s in (2, 1, 3)
    ]
    xw_leaf = [xw_copy(leaf * 16, 16, 2, peer_of(row, col, 1 - leaf))]
    vz_z = [vz_copy(place, 1, 0, peer_of((1 - z_low) * 4 + y, col, leaf))]
    vz_y = [
        vz_copy(y * 2, 2, 1, peer_of(z_low * 4 + (y + s) % 4, col, leaf)) for s in (2, 1, 3)
    ]

    for copy in xw_z + vz_z:
        copy.start()
    pltpu.make_async_copy(child_v, child_v, local_sem.at[0]).wait()
    load_front.start()

    def place_tiles(slot):
        def find(b, found):
            to = col_map[b]
            return tuple(jnp.where(to == slot * 2 + h, b, found[h]) for h in range(2))

        sources = lax.fori_loop(0, 64, find, (0, 0), unroll=8)
        for half, source in enumerate(sources):
            out_v[slot, :, half * TILE : (half + 1) * TILE] = child_v[source]

    def block_copy(m, dz):
        z_to, x_to, leaf_to = (z_high + dz) % 4, (x + m // 2) % 4, (leaf + m % 2) % 2
        slot = (z_to * 4 + x_to) * 2 + leaf_to
        return slot, pltpu.make_async_remote_copy(
            src_ref=out_v.at[slot],
            dst_ref=arrived.at[me],
            send_sem=a2a_send,
            recv_sem=a2a_recv,
            device_id=peer_of(row, z_to * 4 + x_to, leaf_to),
            device_id_type=MESH,
        )

    def send_blocks(first, dz):
        def one(m, carry):
            slot, copy = block_copy(m, dz)
            place_tiles(slot)
            copy.start()
            return carry

        lax.fori_loop(first, 8, one, 0)

    def settle_xw(pieces, stage):
        xw_copy(0, pieces, stage, peer_of(row, col, 1 - leaf)).wait()

    def settle_vz(pieces, stage):
        vz_copy(0, pieces, stage, peer_of(row, col, 1 - leaf)).wait()

    send_blocks(0, 2)
    settle_xw(3, 0)
    settle_vz(1, 0)
    for copy in xw_x + vz_y:
        copy.start()
    send_blocks(0, 1)
    settle_xw(12, 1)
    settle_vz(6, 1)
    for copy in xw_leaf:
        copy.start()
    send_blocks(0, 3)
    send_blocks(1, 0)
    place_tiles(me)
    arrived[me] = out_v[me]
    for copy in small[5:]:
        copy.wait()

    places = lax.broadcasted_iota(jnp.int32, (TILE, TILE), 0)
    chosen = jnp.where(places == pivots[...], jnp.float32(1.0), jnp.float32(0.0))
    permuted = jnp.dot(chosen, dinv[...], precision=HIGHEST, preferred_element_type=jnp.float32)
    z_diag[...] = jnp.zeros_like(z_diag)
    for j in range(2):
        for g in range(8):
            at = (g % 4) * 2 + g // 4
            v_cat[j * RMAX + g * 8 : j * RMAX + g * 8 + 8, :] = vz[at, 0, j]
            z_diag[j * RMAX + g * 8 : j * RMAX + g * 8 + 8, j * TILE : (j + 1) * TILE] = vz[
                at, 1, j
            ]
    dv[...] = lax.dot_general(
        permuted,
        v_cat[...],
        (((1,), (1,)), ((), ())),
        precision=HIGHEST,
        preferred_element_type=jnp.float32,
    )

    settle_xw(16, 2)
    load_front.wait()

    at = lax.broadcasted_iota(jnp.int32, (RMAX, 2 * RMAX), 0)
    piece = at % 32
    rank_row = (piece % 4) * 16 + ((piece // 4) % 4) * 4 + (piece // 16) * 2 + at // 32
    lane = lax.broadcasted_iota(jnp.int32, (RMAX, 2 * RMAX), 1)
    rank_col = lane % RMAX
    second = lane >= RMAX
    limit_col = jnp.where(second, rank_cols[1], rank_cols[0])

    def gathered(first):
        parts = [xw[pl.ds(first + c * 16, 32, stride=64), :] for c in range(4)]
        return jnp.concatenate(
            [jnp.concatenate(parts[:2], axis=1), jnp.concatenate(parts[2:], axis=1)], axis=0
        )

    def tile_row(i, carry):
        x_rows, w_rows = gathered(i), gathered(i + 8)
        core = jnp.dot(w_rows, dv[...], precision=HIGHEST, preferred_element_type=jnp.float32)
        dense = jnp.where(second, admissible[1, i], admissible[0, i]) == 0
        keep = dense | ((rank_row < rank_rows[i]) & (rank_col < limit_col))
        kept = jnp.where(keep, core, jnp.float32(0.0))
        left = lax.dot_general(
            x_rows,
            kept,
            (((0,), (0,)), ((), ())),
            precision=HIGHEST,
            preferred_element_type=jnp.float32,
        )
        update = jnp.dot(
            left, z_diag[...], precision=HIGHEST, preferred_element_type=jnp.float32
        )
        rows = pl.ds(i * 4, 4)
        front_v[rows] = front_v[rows] - update.reshape(4, TILE // 4, 2 * TILE)
        return carry

    lax.fori_loop(0, 8, tile_row, 0)

    pltpu.make_async_remote_copy(
        src_ref=out_v.at[pl.ds(0, 31)],
        dst_ref=arrived.at[pl.ds(0, 31)],
        send_sem=a2a_send,
        recv_sem=a2a_recv,
        device_id=peer_of(row, col, 1 - leaf),
        device_id_type=MESH,
    ).wait()


def place_kernel(row_map, arrived, partial, updated, total, sem):
    copies = []
    for step in range(8 * PARTS):
        to = row_map[0, step // PARTS] * PARTS + step % PARTS
        total[step] = arrived[step] + partial[to]
        copies.append(pltpu.make_async_copy(total.at[step], updated.at[to], sem.at[step]))
        copies[-1].start()
    for copy in copies:
        copy.wait()


def on_device(
    front,
    child,
    row_map,
    col_map,
    x_fac,
    w_fac,
    v_fac,
    z_fac,
    dinv,
    pivots,
    rank_rows,
    rank_cols,
    admissible,
):
    tiles = col_map.shape[0]
    vmem = pl.BlockSpec(memory_space=pltpu.VMEM)
    hbm = pl.BlockSpec(memory_space=pltpu.HBM)
    f32 = jnp.float32
    arrived, partial = pl.pallas_call(
        exchange_kernel,
        name="exchange",
        out_shape=(jax.ShapeDtypeStruct((32, 64, 512), f32),) * 2,
        in_specs=[hbm] * 13,
        out_specs=(vmem, vmem),
        scratch_shapes=[
            pltpu.SMEM((tiles,), jnp.int32),
            pltpu.SMEM(row_map.shape, jnp.int32),
            pltpu.SMEM(rank_rows.shape, jnp.int32),
            pltpu.SMEM(rank_cols.shape, jnp.int32),
            pltpu.SMEM(admissible.shape[::-1], jnp.int32),
            pltpu.VMEM(x_fac.shape, f32),
            pltpu.VMEM(w_fac.shape, f32),
            pltpu.VMEM(v_fac.shape, f32),
            pltpu.VMEM(z_fac.shape, f32),
            pltpu.VMEM(dinv.shape, f32),
            pltpu.VMEM((1, TILE), jnp.int32),
            pltpu.VMEM((tiles, child.shape[0], TILE), f32),
            pltpu.VMEM((32, 64, 512), f32),
            pltpu.VMEM((32 * 64, 128), f32),
            pltpu.VMEM((8, 2, 2, 8, TILE), f32),
            pltpu.VMEM((2 * RMAX, TILE), f32),
            pltpu.VMEM((2 * RMAX, 2 * TILE), f32),
            pltpu.VMEM((TILE, 2 * RMAX), f32),
            pltpu.SemaphoreType.DMA((2,)),
            pltpu.SemaphoreType.DMA((11,)),
            pltpu.SemaphoreType.DMA,
            pltpu.SemaphoreType.DMA,
            pltpu.SemaphoreType.DMA((3,)),
            pltpu.SemaphoreType.DMA((3,)),
            pltpu.SemaphoreType.DMA((2,)),
            pltpu.SemaphoreType.DMA((2,)),
        ],
        compiler_params=pltpu.CompilerParams(
            collective_id=0, has_side_effects=True, vmem_limit_bytes=32 << 20
        ),
    )(*(pltpu.with_memory_space_constraint(a, pltpu.HBM) for a in (
        col_map,
        row_map,
        rank_rows,
        rank_cols,
        admissible.T,
        child,
        front.reshape(32, 64, 512),
        x_fac,
        w_fac,
        v_fac,
        z_fac,
        dinv,
        pivots.reshape(1, TILE),
    )))

    cut = (8 * PARTS, TILE // PARTS, 2 * TILE)
    updated = pl.pallas_call(
        place_kernel,
        name="place_rows",
        out_shape=jax.ShapeDtypeStruct(cut, f32),
        in_specs=[pl.BlockSpec(memory_space=pltpu.SMEM), vmem, vmem],
        out_specs=hbm,
        scratch_shapes=[pltpu.VMEM(cut, f32), pltpu.SemaphoreType.DMA((8 * PARTS,))],
        compiler_params=pltpu.CompilerParams(vmem_limit_bytes=8 << 20),
    )(row_map, arrived.reshape(cut), partial.reshape(cut))
    return updated.reshape(front.shape)


def solution(mesh):
    return jax.shard_map(
        on_device,
        mesh=mesh,
        in_specs=(
            P("row", ("col", "leaf")),
            P(("row", "col", "leaf"), None),
            P("row", None),
            P(),
            P("row", ("col", "leaf")),
            P("row", ("col", "leaf")),
            P(("col", "leaf"), "row"),
            P(("col", "leaf"), "row"),
            P(),
            P(),
            P("row"),
            P(("col", "leaf")),
            P("row", ("col", "leaf")),
        ),
        out_specs=P("row", ("col", "leaf")),
        check_vma=False,
    )
```

```python
import jax
import jax.numpy as jnp
from jax import lax
from jax.experimental import pallas as pl
from jax.experimental.pallas import tpu as pltpu
from jax.sharding import PartitionSpec as P

TILE = 256
RMAX = 64
MESH = pl.DeviceIdType.MESH
PARTS = 2
HIGHEST = lax.Precision.HIGHEST


def peer_of(row, col, leaf):
    return {"row": row, "col": col, "leaf": leaf}


def exchange_kernel(
    col_map_h,
    row_map_h,
    rank_rows_h,
    rank_cols_h,
    admissible_h,
    child,
    front,
    x_fac_h,
    w_fac_h,
    v_fac_h,
    z_fac_h,
    dinv_h,
    pivots_h,
    arrived,
    front_v,
    col_map,
    row_map,
    rank_rows,
    rank_cols,
    admissible,
    x_fac,
    w_fac,
    v_fac,
    z_fac,
    dinv,
    pivots,
    child_v,
    out_v,
    xw,
    vz,
    v_cat,
    z_diag,
    dv,
    local_sem,
    small_sem,
    a2a_send,
    a2a_recv,
    xw_send,
    xw_recv,
    vz_send,
    vz_recv,
):
    row, col, leaf = lax.axis_index("row"), lax.axis_index("col"), lax.axis_index("leaf")
    z_low, y = row // 4, row % 4
    z_high, x = col // 4, col % 4
    me = col * 2 + leaf

    def load_tile(c, carry):
        tile = child.at[:, pl.ds(pl.multiple_of(c * TILE, TILE), TILE)]
        pltpu.make_async_copy(tile, child_v.at[c], local_sem.at[0]).start()
        return carry

    load_front = pltpu.make_async_copy(front, front_v, local_sem.at[1])
    small = [
        pltpu.make_async_copy(source, target, small_sem.at[k])
        for k, (source, target) in enumerate(
            (
                (col_map_h, col_map),
                (x_fac_h, x_fac),
                (w_fac_h, w_fac),
                (v_fac_h, v_fac),
                (z_fac_h, z_fac),
                (dinv_h, dinv),
                (pivots_h, pivots),
                (rank_rows_h, rank_rows),
                (rank_cols_h, rank_cols),
                (admissible_h, admissible),
                (row_map_h, row_map),
            )
        )
    ]
    barrier = pltpu.get_barrier_semaphore()

    xs = [(x + step) % 4 for step in range(4)]
    for dz in (2, 1, 3, 0):
        plane = ((z_high + dz) % 4) * 4
        for m in range(0 if dz else 1, 8):
            to = peer_of(row, plane + xs[m // 2], 1 - leaf if m % 2 else leaf)
            pl.semaphore_signal(barrier, inc=1, device_id=to, device_id_type=MESH)
    pl.semaphore_signal(
        barrier, inc=1, device_id=peer_of((1 - z_low) * 4 + y, col, leaf), device_id_type=MESH
    )
    for step in range(1, 4):
        pl.semaphore_signal(
            barrier,
            inc=1,
            device_id=peer_of(z_low * 4 + (y + step) % 4, col, leaf),
            device_id_type=MESH,
        )

    for copy in small[:5]:
        copy.start()
    lax.fori_loop(0, 64, load_tile, 0, unroll=8)
    for copy in small[5:]:
        copy.start()

    for copy in small[:5]:
        copy.wait()
    spot = leaf * 16 + x * 4 + z_high
    for c in range(4):
        lanes = slice(c * 128, (c + 1) * 128)
        xw[pl.ds(pl.multiple_of(spot * 64 + c * 16, 16), 8), :] = x_fac[:, lanes]
        xw[pl.ds(pl.multiple_of(spot * 64 + c * 16 + 8, 8), 8), :] = w_fac[:, lanes]
    place = y * 2 + z_low
    for q in range(8):
        lanes = slice(q * TILE, (q + 1) * TILE)
        for j in range(2):
            vz[place, 0, j, q : q + 1, :] = v_fac[j : j + 1, lanes]
            vz[place, 1, j, q : q + 1, :] = z_fac[j : j + 1, lanes]

    pl.semaphore_wait(barrier, 35)

    def xw_copy(start, count, stage, to):
        part = xw.at[pl.ds(pl.multiple_of(start * 64, 64), count * 64), :]
        return pltpu.make_async_remote_copy(
            src_ref=part,
            dst_ref=part,
            send_sem=xw_send.at[stage],
            recv_sem=xw_recv.at[stage],
            device_id=to,
            device_id_type=MESH,
        )

    def vz_copy(start, count, stage, to):
        part = vz.at[pl.ds(start, count)]
        return pltpu.make_async_remote_copy(
            src_ref=part,
            dst_ref=part,
            send_sem=vz_send.at[stage],
            recv_sem=vz_recv.at[stage],
            device_id=to,
            device_id_type=MESH,
        )

    xw_z = [
        xw_copy(spot, 1, 0, peer_of(row, ((z_high + s) % 4) * 4 + x, leaf)) for s in (2, 1, 3)
    ]
    xw_x = [
        xw_copy(leaf * 16 + x * 4, 4, 1, peer_of(row, z_high * 4 + (x + s) % 4, leaf))
        for s in (2, 1, 3)
    ]
    xw_leaf = [xw_copy(leaf * 16, 16, 2, peer_of(row, col, 1 - leaf))]
    vz_z = [vz_copy(place, 1, 0, peer_of((1 - z_low) * 4 + y, col, leaf))]
    vz_y = [
        vz_copy(y * 2, 2, 1, peer_of(z_low * 4 + (y + s) % 4, col, leaf)) for s in (2, 1, 3)
    ]

    for copy in xw_z + vz_z:
        copy.start()
    pltpu.make_async_copy(child_v, child_v, local_sem.at[0]).wait()
    load_front.start()

    def place_tiles(slot):
        def find(b, found):
            to = col_map[b]
            return tuple(jnp.where(to == slot * 2 + h, b, found[h]) for h in range(2))

        sources = lax.fori_loop(0, 64, find, (0, 0), unroll=8)
        for half, source in enumerate(sources):
            out_v[slot, :, half * TILE : (half + 1) * TILE] = child_v[source]

    def block_copy(m, dz):
        z_to, x_to, leaf_to = (z_high + dz) % 4, (x + m // 2) % 4, (leaf + m % 2) % 2
        slot = (z_to * 4 + x_to) * 2 + leaf_to
        return slot, pltpu.make_async_remote_copy(
            src_ref=out_v.at[slot],
            dst_ref=arrived.at[me],
            send_sem=a2a_send,
            recv_sem=a2a_recv,
            device_id=peer_of(row, z_to * 4 + x_to, leaf_to),
            device_id_type=MESH,
        )

    def send_blocks(first, dz):
        def one(m, carry):
            slot, copy = block_copy(m, dz)
            place_tiles(slot)
            copy.start()
            return carry

        lax.fori_loop(first, 8, one, 0)

    def settle_xw(pieces, stage):
        xw_copy(0, pieces, stage, peer_of(row, col, 1 - leaf)).wait()

    def settle_vz(pieces, stage):
        vz_copy(0, pieces, stage, peer_of(row, col, 1 - leaf)).wait()

    send_blocks(0, 2)
    settle_xw(3, 0)
    settle_vz(1, 0)
    for copy in xw_x + vz_y:
        copy.start()
    send_blocks(0, 3)
    settle_xw(12, 1)
    settle_vz(6, 1)
    for copy in xw_leaf:
        copy.start()
    send_blocks(0, 1)
    send_blocks(1, 0)
    place_tiles(me)
    arrived[me] = out_v[me]
    for copy in small[5:]:
        copy.wait()

    places = lax.broadcasted_iota(jnp.int32, (TILE, TILE), 0)
    chosen = jnp.where(places == pivots[...], jnp.float32(1.0), jnp.float32(0.0))
    permuted = jnp.dot(chosen, dinv[...], precision=HIGHEST, preferred_element_type=jnp.float32)
    z_diag[...] = jnp.zeros_like(z_diag)
    for j in range(2):
        for g in range(8):
            at = (g % 4) * 2 + g // 4
            v_cat[j * RMAX + g * 8 : j * RMAX + g * 8 + 8, :] = vz[at, 0, j]
            z_diag[j * RMAX + g * 8 : j * RMAX + g * 8 + 8, j * TILE : (j + 1) * TILE] = vz[
                at, 1, j
            ]
    dv[...] = lax.dot_general(
        permuted,
        v_cat[...],
        (((1,), (1,)), ((), ())),
        precision=HIGHEST,
        preferred_element_type=jnp.float32,
    )

    settle_xw(16, 2)
    load_front.wait()

    at = lax.broadcasted_iota(jnp.int32, (RMAX, 2 * RMAX), 0)
    piece = at % 32
    rank_row = (piece % 4) * 16 + ((piece // 4) % 4) * 4 + (piece // 16) * 2 + at // 32
    lane = lax.broadcasted_iota(jnp.int32, (RMAX, 2 * RMAX), 1)
    rank_col = lane % RMAX
    second = lane >= RMAX
    limit_col = jnp.where(second, rank_cols[1], rank_cols[0])

    def gathered(first):
        parts = [xw[pl.ds(first + c * 16, 32, stride=64), :] for c in range(4)]
        return jnp.concatenate(
            [jnp.concatenate(parts[:2], axis=1), jnp.concatenate(parts[2:], axis=1)], axis=0
        )

    def tile_row(i, carry):
        x_rows, w_rows = gathered(i), gathered(i + 8)
        core = jnp.dot(w_rows, dv[...], precision=HIGHEST, preferred_element_type=jnp.float32)
        dense = jnp.where(second, admissible[1, i], admissible[0, i]) == 0
        keep = dense | ((rank_row < rank_rows[i]) & (rank_col < limit_col))
        kept = jnp.where(keep, core, jnp.float32(0.0))
        left = lax.dot_general(
            x_rows,
            kept,
            (((0,), (0,)), ((), ())),
            precision=HIGHEST,
            preferred_element_type=jnp.float32,
        )
        update = jnp.dot(
            left, z_diag[...], precision=HIGHEST, preferred_element_type=jnp.float32
        )
        rows = pl.ds(i * 4, 4)
        front_v[rows] = front_v[rows] - update.reshape(4, TILE // 4, 2 * TILE)
        return carry

    lax.fori_loop(0, 8, tile_row, 0)

    pltpu.make_async_remote_copy(
        src_ref=out_v.at[pl.ds(0, 31)],
        dst_ref=arrived.at[pl.ds(0, 31)],
        send_sem=a2a_send,
        recv_sem=a2a_recv,
        device_id=peer_of(row, col, 1 - leaf),
        device_id_type=MESH,
    ).wait()


def place_kernel(row_map, arrived, partial, updated, total, sem):
    copies = []
    for step in range(8 * PARTS):
        to = row_map[0, step // PARTS] * PARTS + step % PARTS
        total[step] = arrived[step] + partial[to]
        copies.append(pltpu.make_async_copy(total.at[step], updated.at[to], sem.at[step]))
        copies[-1].start()
    for copy in copies:
        copy.wait()


def on_device(
    front,
    child,
    row_map,
    col_map,
    x_fac,
    w_fac,
    v_fac,
    z_fac,
    dinv,
    pivots,
    rank_rows,
    rank_cols,
    admissible,
):
    tiles = col_map.shape[0]
    vmem = pl.BlockSpec(memory_space=pltpu.VMEM)
    hbm = pl.BlockSpec(memory_space=pltpu.HBM)
    f32 = jnp.float32
    arrived, partial = pl.pallas_call(
        exchange_kernel,
        name="exchange",
        out_shape=(jax.ShapeDtypeStruct((32, 64, 512), f32),) * 2,
        in_specs=[hbm] * 13,
        out_specs=(vmem, vmem),
        scratch_shapes=[
            pltpu.SMEM((tiles,), jnp.int32),
            pltpu.SMEM(row_map.shape, jnp.int32),
            pltpu.SMEM(rank_rows.shape, jnp.int32),
            pltpu.SMEM(rank_cols.shape, jnp.int32),
            pltpu.SMEM(admissible.shape[::-1], jnp.int32),
            pltpu.VMEM(x_fac.shape, f32),
            pltpu.VMEM(w_fac.shape, f32),
            pltpu.VMEM(v_fac.shape, f32),
            pltpu.VMEM(z_fac.shape, f32),
            pltpu.VMEM(dinv.shape, f32),
            pltpu.VMEM((1, TILE), jnp.int32),
            pltpu.VMEM((tiles, child.shape[0], TILE), f32),
            pltpu.VMEM((32, 64, 512), f32),
            pltpu.VMEM((32 * 64, 128), f32),
            pltpu.VMEM((8, 2, 2, 8, TILE), f32),
            pltpu.VMEM((2 * RMAX, TILE), f32),
            pltpu.VMEM((2 * RMAX, 2 * TILE), f32),
            pltpu.VMEM((TILE, 2 * RMAX), f32),
            pltpu.SemaphoreType.DMA((2,)),
            pltpu.SemaphoreType.DMA((11,)),
            pltpu.SemaphoreType.DMA,
            pltpu.SemaphoreType.DMA,
            pltpu.SemaphoreType.DMA((3,)),
            pltpu.SemaphoreType.DMA((3,)),
            pltpu.SemaphoreType.DMA((2,)),
            pltpu.SemaphoreType.DMA((2,)),
        ],
        compiler_params=pltpu.CompilerParams(
            collective_id=0, has_side_effects=True, vmem_limit_bytes=32 << 20
        ),
    )(*(pltpu.with_memory_space_constraint(a, pltpu.HBM) for a in (
        col_map,
        row_map,
        rank_rows,
        rank_cols,
        admissible.T,
        child,
        front.reshape(32, 64, 512),
        x_fac,
        w_fac,
        v_fac,
        z_fac,
        dinv,
        pivots.reshape(1, TILE),
    )))

    cut = (8 * PARTS, TILE // PARTS, 2 * TILE)
    updated = pl.pallas_call(
        place_kernel,
        name="place_rows",
        out_shape=jax.ShapeDtypeStruct(cut, f32),
        in_specs=[pl.BlockSpec(memory_space=pltpu.SMEM), vmem, vmem],
        out_specs=hbm,
        scratch_shapes=[pltpu.VMEM(cut, f32), pltpu.SemaphoreType.DMA((8 * PARTS,))],
        compiler_params=pltpu.CompilerParams(vmem_limit_bytes=8 << 20),
    )(row_map, arrived.reshape(cut), partial.reshape(cut))
    return updated.reshape(front.shape)


def solution(mesh):
    return jax.shard_map(
        on_device,
        mesh=mesh,
        in_specs=(
            P("row", ("col", "leaf")),
            P(("row", "col", "leaf"), None),
            P("row", None),
            P(),
            P("row", ("col", "leaf")),
            P("row", ("col", "leaf")),
            P(("col", "leaf"), "row"),
            P(("col", "leaf"), "row"),
            P(),
            P(),
            P("row"),
            P(("col", "leaf")),
            P("row", ("col", "leaf")),
        ),
        out_specs=P("row", ("col", "leaf")),
        check_vma=False,
    )
```

```python
import jax
import jax.numpy as jnp
from jax import lax
from jax.experimental import pallas as pl
from jax.experimental.pallas import tpu as pltpu
from jax.sharding import PartitionSpec as P

TILE = 256
RMAX = 64
MESH = pl.DeviceIdType.MESH
PARTS = 2
HIGHEST = lax.Precision.HIGHEST


def peer_of(row, col, leaf):
    return {"row": row, "col": col, "leaf": leaf}


def exchange_kernel(
    col_map_h,
    row_map_h,
    rank_rows_h,
    rank_cols_h,
    admissible_h,
    child,
    front,
    x_fac_h,
    w_fac_h,
    v_fac_h,
    z_fac_h,
    dinv_h,
    pivots_h,
    arrived,
    front_v,
    col_map,
    row_map,
    rank_rows,
    rank_cols,
    admissible,
    x_fac,
    w_fac,
    v_fac,
    z_fac,
    dinv,
    pivots,
    child_v,
    out_v,
    xw,
    vz,
    v_cat,
    z_diag,
    dv,
    local_sem,
    small_sem,
    a2a_send,
    a2a_recv,
    xw_send,
    xw_recv,
    vz_send,
    vz_recv,
):
    row, col, leaf = lax.axis_index("row"), lax.axis_index("col"), lax.axis_index("leaf")
    z_low, y = row // 4, row % 4
    z_high, x = col // 4, col % 4
    me = col * 2 + leaf

    def load_tile(c, carry):
        tile = child.at[:, pl.ds(pl.multiple_of(c * TILE, TILE), TILE)]
        pltpu.make_async_copy(tile, child_v.at[c], local_sem.at[0]).start()
        return carry

    load_front = pltpu.make_async_copy(front, front_v, local_sem.at[1])
    small = [
        pltpu.make_async_copy(source, target, small_sem.at[k])
        for k, (source, target) in enumerate(
            (
                (col_map_h, col_map),
                (x_fac_h, x_fac),
                (w_fac_h, w_fac),
                (v_fac_h, v_fac),
                (z_fac_h, z_fac),
                (dinv_h, dinv),
                (pivots_h, pivots),
                (rank_rows_h, rank_rows),
                (rank_cols_h, rank_cols),
                (admissible_h, admissible),
                (row_map_h, row_map),
            )
        )
    ]
    barrier = pltpu.get_barrier_semaphore()

    xs = [(x + step) % 4 for step in range(4)]
    for dz in (2, 1, 3, 0):
        plane = ((z_high + dz) % 4) * 4
        for m in range(0 if dz else 1, 8):
            to = peer_of(row, plane + xs[m // 2], 1 - leaf if m % 2 else leaf)
            pl.semaphore_signal(barrier, inc=1, device_id=to, device_id_type=MESH)
    pl.semaphore_signal(
        barrier, inc=1, device_id=peer_of((1 - z_low) * 4 + y, col, leaf), device_id_type=MESH
    )
    for step in range(1, 4):
        pl.semaphore_signal(
            barrier,
            inc=1,
            device_id=peer_of(z_low * 4 + (y + step) % 4, col, leaf),
            device_id_type=MESH,
        )

    for copy in small[:5]:
        copy.start()
    lax.fori_loop(0, 64, load_tile, 0, unroll=16)
    for copy in small[5:]:
        copy.start()

    for copy in small[:5]:
        copy.wait()
    spot = leaf * 16 + x * 4 + z_high
    for c in range(4):
        lanes = slice(c * 128, (c + 1) * 128)
        xw[pl.ds(pl.multiple_of(spot * 64 + c * 16, 16), 8), :] = x_fac[:, lanes]
        xw[pl.ds(pl.multiple_of(spot * 64 + c * 16 + 8, 8), 8), :] = w_fac[:, lanes]
    place = y * 2 + z_low
    for q in range(8):
        lanes = slice(q * TILE, (q + 1) * TILE)
        for j in range(2):
            vz[place, 0, j, q : q + 1, :] = v_fac[j : j + 1, lanes]
            vz[place, 1, j, q : q + 1, :] = z_fac[j : j + 1, lanes]

    pl.semaphore_wait(barrier, 35)

    def xw_copy(start, count, stage, to):
        part = xw.at[pl.ds(pl.multiple_of(start * 64, 64), count * 64), :]
        return pltpu.make_async_remote_copy(
            src_ref=part,
            dst_ref=part,
            send_sem=xw_send.at[stage],
            recv_sem=xw_recv.at[stage],
            device_id=to,
            device_id_type=MESH,
        )

    def vz_copy(start, count, stage, to):
        part = vz.at[pl.ds(start, count)]
        return pltpu.make_async_remote_copy(
            src_ref=part,
            dst_ref=part,
            send_sem=vz_send.at[stage],
            recv_sem=vz_recv.at[stage],
            device_id=to,
            device_id_type=MESH,
        )

    xw_z = [
        xw_copy(spot, 1, 0, peer_of(row, ((z_high + s) % 4) * 4 + x, leaf)) for s in (2, 1, 3)
    ]
    xw_x = [
        xw_copy(leaf * 16 + x * 4, 4, 1, peer_of(row, z_high * 4 + (x + s) % 4, leaf))
        for s in (2, 1, 3)
    ]
    xw_leaf = [xw_copy(leaf * 16, 16, 2, peer_of(row, col, 1 - leaf))]
    vz_z = [vz_copy(place, 1, 0, peer_of((1 - z_low) * 4 + y, col, leaf))]
    vz_y = [
        vz_copy(y * 2, 2, 1, peer_of(z_low * 4 + (y + s) % 4, col, leaf)) for s in (2, 1, 3)
    ]

    for copy in xw_z + vz_z:
        copy.start()
    pltpu.make_async_copy(child_v, child_v, local_sem.at[0]).wait()
    load_front.start()

    def place_tiles(slot):
        def find(b, found):
            to = col_map[b]
            return tuple(jnp.where(to == slot * 2 + h, b, found[h]) for h in range(2))

        sources = lax.fori_loop(0, 64, find, (0, 0), unroll=8)
        for half, source in enumerate(sources):
            out_v[slot, :, half * TILE : (half + 1) * TILE] = child_v[source]

    def block_copy(m, dz):
        z_to, x_to, leaf_to = (z_high + dz) % 4, (x + m // 2) % 4, (leaf + m % 2) % 2
        slot = (z_to * 4 + x_to) * 2 + leaf_to
        return slot, pltpu.make_async_remote_copy(
            src_ref=out_v.at[slot],
            dst_ref=arrived.at[me],
            send_sem=a2a_send,
            recv_sem=a2a_recv,
            device_id=peer_of(row, z_to * 4 + x_to, leaf_to),
            device_id_type=MESH,
        )

    def send_blocks(first, dz):
        def one(m, carry):
            slot, copy = block_copy(m, dz)
            place_tiles(slot)
            copy.start()
            return carry

        lax.fori_loop(first, 8, one, 0)

    def settle_xw(pieces, stage):
        xw_copy(0, pieces, stage, peer_of(row, col, 1 - leaf)).wait()

    def settle_vz(pieces, stage):
        vz_copy(0, pieces, stage, peer_of(row, col, 1 - leaf)).wait()

    send_blocks(0, 2)
    settle_xw(3, 0)
    settle_vz(1, 0)
    for copy in xw_x + vz_y:
        copy.start()
    send_blocks(0, 3)
    settle_xw(12, 1)
    settle_vz(6, 1)
    for copy in xw_leaf:
        copy.start()
    send_blocks(0, 1)
    send_blocks(1, 0)
    place_tiles(me)
    arrived[me] = out_v[me]
    for copy in small[5:]:
        copy.wait()

    places = lax.broadcasted_iota(jnp.int32, (TILE, TILE), 0)
    chosen = jnp.where(places == pivots[...], jnp.float32(1.0), jnp.float32(0.0))
    permuted = jnp.dot(chosen, dinv[...], precision=HIGHEST, preferred_element_type=jnp.float32)
    z_diag[...] = jnp.zeros_like(z_diag)
    for j in range(2):
        for g in range(8):
            at = (g % 4) * 2 + g // 4
            v_cat[j * RMAX + g * 8 : j * RMAX + g * 8 + 8, :] = vz[at, 0, j]
            z_diag[j * RMAX + g * 8 : j * RMAX + g * 8 + 8, j * TILE : (j + 1) * TILE] = vz[
                at, 1, j
            ]
    dv[...] = lax.dot_general(
        permuted,
        v_cat[...],
        (((1,), (1,)), ((), ())),
        precision=HIGHEST,
        preferred_element_type=jnp.float32,
    )

    settle_xw(16, 2)
    load_front.wait()

    at = lax.broadcasted_iota(jnp.int32, (RMAX, 2 * RMAX), 0)
    piece = at % 32
    rank_row = (piece % 4) * 16 + ((piece // 4) % 4) * 4 + (piece // 16) * 2 + at // 32
    lane = lax.broadcasted_iota(jnp.int32, (RMAX, 2 * RMAX), 1)
    rank_col = lane % RMAX
    second = lane >= RMAX
    limit_col = jnp.where(second, rank_cols[1], rank_cols[0])

    def gathered(first):
        parts = [xw[pl.ds(first + c * 16, 32, stride=64), :] for c in range(4)]
        return jnp.concatenate(
            [jnp.concatenate(parts[:2], axis=1), jnp.concatenate(parts[2:], axis=1)], axis=0
        )

    def tile_row(i, carry):
        x_rows, w_rows = gathered(i), gathered(i + 8)
        core = jnp.dot(w_rows, dv[...], precision=HIGHEST, preferred_element_type=jnp.float32)
        dense = jnp.where(second, admissible[1, i], admissible[0, i]) == 0
        keep = dense | ((rank_row < rank_rows[i]) & (rank_col < limit_col))
        kept = jnp.where(keep, core, jnp.float32(0.0))
        left = lax.dot_general(
            x_rows,
            kept,
            (((0,), (0,)), ((), ())),
            precision=HIGHEST,
            preferred_element_type=jnp.float32,
        )
        update = jnp.dot(
            left, z_diag[...], precision=HIGHEST, preferred_element_type=jnp.float32
        )
        rows = pl.ds(i * 4, 4)
        front_v[rows] = front_v[rows] - update.reshape(4, TILE // 4, 2 * TILE)
        return carry

    lax.fori_loop(0, 8, tile_row, 0)

    pltpu.make_async_remote_copy(
        src_ref=out_v.at[pl.ds(0, 31)],
        dst_ref=arrived.at[pl.ds(0, 31)],
        send_sem=a2a_send,
        recv_sem=a2a_recv,
        device_id=peer_of(row, col, 1 - leaf),
        device_id_type=MESH,
    ).wait()


def place_kernel(row_map, arrived, partial, updated, total, sem):
    copies = []
    for step in range(8 * PARTS):
        to = row_map[0, step // PARTS] * PARTS + step % PARTS
        total[step] = arrived[step] + partial[to]
        copies.append(pltpu.make_async_copy(total.at[step], updated.at[to], sem.at[step]))
        copies[-1].start()
    for copy in copies:
        copy.wait()


def on_device(
    front,
    child,
    row_map,
    col_map,
    x_fac,
    w_fac,
    v_fac,
    z_fac,
    dinv,
    pivots,
    rank_rows,
    rank_cols,
    admissible,
):
    tiles = col_map.shape[0]
    vmem = pl.BlockSpec(memory_space=pltpu.VMEM)
    hbm = pl.BlockSpec(memory_space=pltpu.HBM)
    f32 = jnp.float32
    arrived, partial = pl.pallas_call(
        exchange_kernel,
        name="exchange",
        out_shape=(jax.ShapeDtypeStruct((32, 64, 512), f32),) * 2,
        in_specs=[hbm] * 13,
        out_specs=(vmem, vmem),
        scratch_shapes=[
            pltpu.SMEM((tiles,), jnp.int32),
            pltpu.SMEM(row_map.shape, jnp.int32),
            pltpu.SMEM(rank_rows.shape, jnp.int32),
            pltpu.SMEM(rank_cols.shape, jnp.int32),
            pltpu.SMEM(admissible.shape[::-1], jnp.int32),
            pltpu.VMEM(x_fac.shape, f32),
            pltpu.VMEM(w_fac.shape, f32),
            pltpu.VMEM(v_fac.shape, f32),
            pltpu.VMEM(z_fac.shape, f32),
            pltpu.VMEM(dinv.shape, f32),
            pltpu.VMEM((1, TILE), jnp.int32),
            pltpu.VMEM((tiles, child.shape[0], TILE), f32),
            pltpu.VMEM((32, 64, 512), f32),
            pltpu.VMEM((32 * 64, 128), f32),
            pltpu.VMEM((8, 2, 2, 8, TILE), f32),
            pltpu.VMEM((2 * RMAX, TILE), f32),
            pltpu.VMEM((2 * RMAX, 2 * TILE), f32),
            pltpu.VMEM((TILE, 2 * RMAX), f32),
            pltpu.SemaphoreType.DMA((2,)),
            pltpu.SemaphoreType.DMA((11,)),
            pltpu.SemaphoreType.DMA,
            pltpu.SemaphoreType.DMA,
            pltpu.SemaphoreType.DMA((3,)),
            pltpu.SemaphoreType.DMA((3,)),
            pltpu.SemaphoreType.DMA((2,)),
            pltpu.SemaphoreType.DMA((2,)),
        ],
        compiler_params=pltpu.CompilerParams(
            collective_id=0, has_side_effects=True, vmem_limit_bytes=32 << 20
        ),
    )(*(pltpu.with_memory_space_constraint(a, pltpu.HBM) for a in (
        col_map,
        row_map,
        rank_rows,
        rank_cols,
        admissible.T,
        child,
        front.reshape(32, 64, 512),
        x_fac,
        w_fac,
        v_fac,
        z_fac,
        dinv,
        pivots.reshape(1, TILE),
    )))

    cut = (8 * PARTS, TILE // PARTS, 2 * TILE)
    updated = pl.pallas_call(
        place_kernel,
        name="place_rows",
        out_shape=jax.ShapeDtypeStruct(cut, f32),
        in_specs=[pl.BlockSpec(memory_space=pltpu.SMEM), vmem, vmem],
        out_specs=hbm,
        scratch_shapes=[pltpu.VMEM(cut, f32), pltpu.SemaphoreType.DMA((8 * PARTS,))],
        compiler_params=pltpu.CompilerParams(vmem_limit_bytes=8 << 20),
    )(row_map, arrived.reshape(cut), partial.reshape(cut))
    return updated.reshape(front.shape)


def solution(mesh):
    return jax.shard_map(
        on_device,
        mesh=mesh,
        in_specs=(
            P("row", ("col", "leaf")),
            P(("row", "col", "leaf"), None),
            P("row", None),
            P(),
            P("row", ("col", "leaf")),
            P("row", ("col", "leaf")),
            P(("col", "leaf"), "row"),
            P(("col", "leaf"), "row"),
            P(),
            P(),
            P("row"),
            P(("col", "leaf")),
            P("row", ("col", "leaf")),
        ),
        out_specs=P("row", ("col", "leaf")),
        check_vma=False,
    )
```
